32 devices in a mesh: groups: 2 (over x), mset: 16 (over z, y, core).
Axes of the slice: x: 2, y: 2, z: 4, core: 2. Of those that a mesh axis runs over, the one named last changes fastest.
Arguments:
- m_list: int32 [16], replicated, may hold values from 1536 to 3071, as said below
- coeff: bfloat16 [32, 32, 1536], P(('groups', 'mset')), parts along dimension 0, may hold values from -6 to 6
- blocks: bfloat16 [32, 1536, 1536], P(('groups', 'mset')), parts along dimension 0, may hold values from -0.15625 to 0.15625
- legendre: bfloat16 [512, 16, 1536], P(('groups', 'mset')), parts along dimension 0, may hold values from -0.15625 to 0.15625
Outputs:
- sky_map: bfloat16 [512, 16, 8192], P(('groups', 'mset')), parts along dimension 0
The draws below stay inside these ranges and needn't reach their ends.
There are 2 independent parts, one for each index of `groups`. The reference program is written for one: setup_inputs(seed, part) draws one part's arguments, and reference() takes and returns one part's arrays. A program takes and returns all parts, laid end to end along the dimension named above; an argument that names none is the same for every part. Nothing has to cross between parts.
Inputs may be any that keep to these rules, and one draw needn't show every extreme that they name: `m_list`: 16 distinct values; the value 3072 - 1536, a block of full order 1536, is always among them.
All inputs are finite; a program needn't handle non-finite values.
Results may differ from the reference program's by a relative error of at most 0.0062.
Values may be sent and summed in bfloat16 or wider, within the bound.
A program may use at most 64 MiB of HBM per device.

```python
import math
import jax
import jax.numpy as jnp
from jax import lax

LL = 3072
LB = 1536
REAL = 16
COLS = 32
NPHI = 8192
M_SUB = 16
CYCLES = 256


def draw_m_list(key, part):
    shuffled = jax.random.permutation(jax.random.fold_in(key, 11), LB).astype(jnp.int32)
    target = jax.random.randint(jax.random.fold_in(key, 12), (), 0, M_SUB).astype(jnp.int32)
    zero_pos = jnp.argmax(shuffled == 0).astype(jnp.int32)
    moved_value = shuffled[target]
    shuffled = shuffled.at[zero_pos].set(moved_value)
    shuffled = shuffled.at[target].set(jnp.int32(0))
    return (LL - LB + shuffled[:M_SUB]).astype(jnp.int32)


def shard_levels(rng, shape, shards, least, high):
    def one(dim, parts):
        heights = jax.random.uniform(jax.random.fold_in(jax.random.fold_in(rng, 6), dim), (parts,), jnp.float32, least / len(shards), high / len(shards))
        return jnp.repeat(jnp.exp(heights), shape[dim] // parts).reshape((-1,) + (1,) * (len(shape) - dim - 1))

    level = one(*shards[0])
    for cut in shards[1:]:
        level = level * one(*cut)
    return level


def scatter_about(own_key, dims, scale, bound, pieces=(), kind=jnp.bfloat16):
    gain = shard_levels(own_key, dims, pieces, -0.22, 0.18) if pieces else 1.0
    array = jax.random.normal(own_key, dims, jnp.float32) * scale * gain
    return jnp.minimum(jnp.maximum(array, -bound), bound).astype(kind)


def setup_inputs(seed: int = 0, part: int = 0) -> dict:
    arg_keys = jax.random.split(jax.random.key(seed), 5)
    part_keys = jax.random.split(jax.random.fold_in(arg_keys[4], part), 5)
    return {
        "m_list": draw_m_list(jax.random.fold_in(arg_keys[4], 71), part),
        "coeff": scatter_about(part_keys[1], (M_SUB, COLS, LB), 1.0, 6.0, ((0, 16),)),
        "blocks": scatter_about(part_keys[2], (M_SUB, LB, LB), LB ** -0.5, 0.15625, ((0, 16),)),
        "legendre": scatter_about(part_keys[3], (CYCLES, M_SUB, LB), LB ** -0.5, 0.15625, ((0, 16),)),
    }


def fourier_table(m_values, pixels):
    pixel_index = jnp.arange(pixels, dtype=jnp.int32)
    phases = m_values.astype(jnp.int32)[:, None] * pixel_index[None, :] % pixels
    angles = phases.astype(jnp.float32) * (2.0 * math.pi / pixels)
    cos_part = jnp.cos(angles).astype(jnp.bfloat16)
    sin_part = jnp.sin(angles).astype(jnp.bfloat16)
    return jnp.concatenate([cos_part, -sin_part], axis=0)

def reference(m_list, coeff, blocks, legendre):
    orders = (LL - m_list).astype(jnp.int32)
    valid_mask = jnp.arange(LB, dtype=jnp.int32)[None, :] < orders[:, None]

    def block_apply(items):
        column_block, inverse, valid_row = items
        masked = jnp.where(valid_row[None, :], column_block, jnp.zeros_like(column_block))
        products = jnp.dot(masked.astype(jnp.float32), inverse.astype(jnp.float32), preferred_element_type=jnp.float32)
        return jnp.where(valid_row[None, :], products, jnp.zeros_like(products)).astype(jnp.bfloat16)
    filtered = lax.map(block_apply, (coeff, blocks, valid_mask))
    filtered_wide = filtered.astype(jnp.float32)

    def cycle_sum(cycle_table):
        return jnp.einsum('mj,mcj->mc', cycle_table.astype(jnp.float32), filtered_wide).astype(jnp.bfloat16)
    harmonics = lax.map(cycle_sum, legendre)
    real_part = harmonics[:, :, :REAL]
    imag_part = harmonics[:, :, REAL:]
    stacked = jnp.concatenate([real_part, imag_part], axis=1)
    flattened = jnp.transpose(stacked, (0, 2, 1)).reshape(CYCLES * REAL, 2 * M_SUB)
    trig_table = fourier_table(m_list, NPHI)
    summed = jnp.dot(flattened.astype(jnp.float32), trig_table.astype(jnp.float32), preferred_element_type=jnp.float32)
    scaled = summed * (1.0 / math.sqrt(M_SUB))
    return scaled.astype(jnp.bfloat16).reshape(CYCLES, REAL, NPHI)
```

```python
import functools
import math

import jax
import jax.numpy as jnp
from jax import lax
from jax.experimental import pallas as pl
from jax.experimental.pallas import tpu as pltpu
from jax.sharding import PartitionSpec as P

LL = 3072
REAL = 16
NPHI = 8192
LANES = 128
MESH = pl.DeviceIdType.MESH
F32 = jnp.float32
BF16 = jnp.bfloat16


def iota(shape, dim):
    return lax.broadcasted_iota(jnp.int32, shape, dim)


def split_index(x, size):
    if size & (size - 1) == 0:
        shift = size.bit_length() - 1
        return lax.shift_right_logical(x, jnp.int32(shift)), lax.bitwise_and(x, jnp.int32(size - 1))
    quotient = x // size
    return quotient, x - quotient * size


def fill_table(m_s, table):
    subset = m_s.shape[0]
    m_col = jnp.zeros((subset, LANES), jnp.int32)
    slot = iota((subset, LANES), 0)
    for i in range(subset):
        m_col = jnp.where(slot == i, m_s[i], m_col)
    lane = iota((subset, LANES), 1)
    fine = split_index(m_col * lane, NPHI)[1].astype(F32) * (2.0 * math.pi / NPHI)
    coarse = split_index(m_col * (lane * LANES), NPHI)[1].astype(F32) * (2.0 * math.pi / NPHI)
    fine_cos, fine_sin = jnp.cos(fine), jnp.sin(fine)
    coarse_cos, coarse_sin = jnp.cos(coarse), jnp.sin(coarse)
    for a in range(NPHI // LANES):
        c = coarse_cos[:, a : a + 1]
        s = coarse_sin[:, a : a + 1]
        table[0:subset, a * LANES : (a + 1) * LANES] = (c * fine_cos - s * fine_sin).astype(BF16)
        table[subset : 2 * subset, a * LANES : (a + 1) * LANES] = (-(s * fine_cos + c * fine_sin)).astype(BF16)


def harmonics_kernel(
    n, chunks, m_ref, coeff_ref, blocks_ref, leg_ref, out_ref, table_ref,
    m_s, coeff_v, blocks_v, leg_v, leg_p, legs, legx, gathered, crossed, harm_s, harm_x, harm_r,
    load_sem, recv_sem, up_sem, down_sem, cross_send, cross_recv, next_send,
    sib_sem, zsib_sem, far_send, far_recv, quad_sem, turn_send, turn_recv, harm_send, harm_recv,
):
    subset = m_ref.shape[0]
    cols, order_max = coeff_ref.shape[1], coeff_ref.shape[2]
    width = order_max // chunks
    group = 4
    depth = n // group
    far = depth - 2
    rows_in = leg_ref.shape[0]
    rows_out = out_ref.shape[0]
    cycles = rows_in // subset
    span = depth * cols
    me = lax.axis_index("mset")
    core = lax.rem(me, 2)
    side = lax.rem(lax.div(me, 2), 2)
    z = lax.div(me, group)
    sibling = me + 1 - 2 * core
    partner = me + 2 - 4 * side
    diagonal = sibling + 2 - 4 * side
    odd = lax.rem(z, 2)
    mate_z = z + 1 - 2 * odd
    mate = me + group - 2 * group * odd
    mate_sib = sibling + group - 2 * group * odd
    upper = z >= depth // 2
    outer = jnp.where(upper, odd == 1, odd == 0)
    inner = jnp.logical_not(outer)
    pair_lo = z - odd

    def remote(src, dst, send_sem, recv_sem_, target):
        return pltpu.make_async_remote_copy(
            src_ref=src, dst_ref=dst, send_sem=send_sem, recv_sem=recv_sem_,
            device_id={"mset": target}, device_id_type=MESH,
        )

    def load_block(q):
        return pltpu.make_async_copy(
            blocks_ref.at[0, :, pl.ds(q * width, width)], blocks_v.at[q], load_sem.at[q]
        )

    m_load = pltpu.make_async_copy(m_ref, m_s, load_sem.at[chunks + 2])
    coeff_load = pltpu.make_async_copy(coeff_ref.at[0], coeff_v, load_sem.at[chunks])
    leg_load = pltpu.make_async_copy(leg_ref, leg_v, load_sem.at[chunks + 1])
    m_load.start()
    coeff_load.start()
    load_block(0).start()
    leg_load.start()
    for q in range(1, chunks):
        load_block(q).start()

    barrier = pltpu.get_barrier_semaphore()

    def greet(target):
        pl.semaphore_signal(barrier, inc=1, device_id={"mset": target}, device_id_type=MESH)

    greet(sibling)
    greet(partner)
    greet(diagonal)
    greet(mate_sib)

    @pl.when(z > 0)
    def _():
        greet(me - group)

    @pl.when(z < depth - 1)
    def _():
        greet(me + group)

    def to_up(zz, q):
        piece = gathered.at[q, zz]
        return remote(piece, piece, up_sem.at[q, zz], recv_sem.at[q, zz], me + group)

    def to_down(zz, q):
        piece = gathered.at[q, zz]
        return remote(piece, piece, down_sem.at[q, zz], recv_sem.at[q, zz], me - group)

    def arrive(zz, q):
        piece = gathered.at[q, zz]
        remote(piece, piece, up_sem.at[q, 0], recv_sem.at[q, zz], sibling).wait_recv()

    def to_cross(q):
        return remote(gathered.at[q, z], crossed.at[q, 0], cross_send.at[q], cross_recv.at[q, 0], partner)

    def to_next(q):
        return remote(crossed.at[q, 0], crossed.at[q, 1], next_send.at[q], cross_recv.at[q, 1], mate)

    leg_sib = remote(leg_p.at[0], legs.at[pl.ds(depth, depth)], sib_sem.at[0], sib_sem.at[1], sibling)
    leg_zsib = remote(leg_p.at[2, z], legx.at[0], zsib_sem.at[0], zsib_sem.at[1], sibling)

    def far_z(k):
        return k + jnp.where(k >= pair_lo, 2, 0)

    def leg_far(lane, k):
        target = diagonal if lane else partner
        return remote(
            leg_p.at[1 + lane, far_z(k)], legs.at[2 * depth + lane * far + k],
            far_send.at[lane, k], far_recv.at[lane, k], target,
        )

    leg_quad = remote(leg_p.at[1, mate_z], legx.at[1], quad_sem.at[0], quad_sem.at[1], mate)
    turn_slot = jnp.where(outer, 0, 1)
    leg_turn = remote(
        leg_p.at[2, mate_z], legx.at[2 + turn_slot], turn_send.at[0], turn_recv.at[turn_slot],
        jnp.where(outer, mate_sib, sibling),
    )

    m_load.wait()
    order = LL - m_s[me]
    coeff_load.wait()
    masked = jnp.where(iota((cols, order_max), 1) < order, coeff_v[...].astype(F32), 0.0).astype(BF16)

    def filter_chunk(q):
        load_block(q).wait()
        product = jnp.dot(masked, blocks_v[q], preferred_element_type=F32)
        valid = iota((cols, width), 1) + q * width < order
        gathered[q, z] = jnp.where(valid, product, 0.0).astype(BF16)

        if q == 0:
            peers = 4 + jnp.where(z > 0, 1, 0) + jnp.where(z < depth - 1, 1, 0)
            pl.semaphore_wait(barrier, peers)

        @pl.when(z < depth - 1)
        def _():
            to_up(z, q).start()

        @pl.when(z > 0)
        def _():
            to_down(z, q).start()

        to_cross(q).start()

    filter_chunk(0)

    rows_all = group * depth * cycles
    row_class, row_rest = split_index(iota((rows_all, rows_in), 0), depth * cycles)
    row_z, row_cycle = split_index(row_rest, cycles)
    row_dy, row_dc = split_index(row_class, 2)
    row_y = jnp.where(row_dy == 1, 1 - side, side)
    row_c = jnp.where(row_dc == 1, 1 - core, core)
    wanted = row_cycle * subset + row_z * group + row_y * 2 + row_c
    permute = jnp.where(iota((rows_all, rows_in), 1) == wanted, 1.0, 0.0).astype(BF16)
    leg_load.wait()
    for q in range(chunks):
        cut = slice(q * width, (q + 1) * width)
        moved = jnp.dot(permute, leg_v[:, cut], preferred_element_type=F32).astype(BF16)
        moved = moved.reshape(group, depth, cycles, width)
        legs[0:depth, :, cut] = moved[0]
        leg_p[:, :, :, cut] = moved[1:]

    for q in range(1, chunks):
        filter_chunk(q)

    for k in range(far):
        for lane in range(2):
            leg_far(lane, k).start()

    @pl.when(outer)
    def _():
        leg_quad.start()

    leg_turn.start()
    leg_sib.start()
    leg_zsib.start()

    fill_table(m_s, table_ref)

    def below(d, q):
        arrive(z - d, q)

        @pl.when(z < depth - 1)
        def _():
            to_up(z - d, q).start()

    def above(d, q):
        arrive(z + d, q)

        @pl.when(z > 0)
        def _():
            to_down(z + d, q).start()

    def cross_arrive(q):
        to_cross(q).wait_recv()

        @pl.when(outer)
        def _():
            to_next(q).start()

    def relay(d, q):
        pl.when(z >= d)(functools.partial(below, d, q))
        pl.when(z <= depth - 1 - d)(functools.partial(above, d, q))

    for d in range(1, depth - 1):
        for q in range(chunks):
            relay(d, q)
            if d == 1:
                cross_arrive(q)

    lane_z = split_index(iota((cycles, span), 1), cols)[0]

    def at_z(x, zz):
        return jnp.where(lane_z == zz, x, 0.0)

    contract_last = (((1,), (1,)), ((), ()))

    def meet(rows, slot):
        total = jnp.zeros((rows.shape[0], span), F32)
        for q in range(chunks):
            f = crossed[q, slot]
            total += lax.dot_general(
                rows[:, q * width : (q + 1) * width], jnp.concatenate([f] * depth, axis=0),
                contract_last, preferred_element_type=F32,
            )
        return total

    def harm_copy(src, slot, target):
        return remote(src, harm_r.at[slot], harm_send.at[slot], harm_recv.at[slot], target)

    to_sib = harm_copy(harm_s.at[0], 0, sibling)
    to_partner = harm_copy(harm_s.at[1], 1, partner)
    to_diag = harm_copy(harm_s.at[2], 2, diagonal)
    to_sib_x = harm_copy(harm_x.at[1], 3, sibling)
    to_mate = harm_copy(harm_x.at[2], 4, mate)
    to_mate_sib = harm_copy(harm_x.at[3], 5, mate_sib)

    leg_zsib.wait_recv()

    @pl.when(outer)
    def _():
        x = meet(jnp.concatenate([leg_p[1, z], legx[0]], axis=0), 0)
        harm_x[0] = at_z(x[0:cycles], z).astype(BF16)
        harm_x[1] = at_z(x[cycles : 2 * cycles], z).astype(BF16)
        to_sib_x.start()

    leg_sib.wait_recv()
    total_rows = (2 * depth + 2 * far) * cycles
    cross = jnp.zeros((total_rows, span), F32)
    for q in range(chunks):
        relay(depth - 1, q)
        if q == 0:
            for k in range(far):
                for lane in range(2):
                    leg_far(lane, k).wait_recv()
        cross += lax.dot_general(
            legs[:, :, q * width : (q + 1) * width].reshape(total_rows, width),
            gathered[q].reshape(span, width),
            contract_last, preferred_element_type=F32,
        )

    def collect(first, zs):
        out = jnp.zeros((cycles, span), F32)
        for k, zz in enumerate(zs):
            out += at_z(cross[(first + k) * cycles : (first + k + 1) * cycles], zz)
        return out.astype(BF16)

    far_list = [far_z(k) for k in range(far)]
    harm_s[1] = collect(2 * depth, far_list)
    to_partner.start()
    harm_s[2] = collect(2 * depth + far, far_list)
    to_diag.start()
    harm_s[0] = collect(depth, range(depth))
    to_sib.start()
    own = collect(0, range(depth))

    @pl.when(inner)
    def _():
        leg_quad.wait_recv()
        for slot in range(2):
            remote(leg_p.at[2, mate_z], legx.at[2 + slot], turn_send.at[0], turn_recv.at[slot], sibling).wait_recv()
        x = meet(jnp.concatenate([leg_p[1, z], legx[0], legx[1], legx[2]], axis=0), 0)
        harm_x[2] = at_z(x[2 * cycles : 3 * cycles], z).astype(BF16)
        to_mate.start()
        harm_x[3] = at_z(x[3 * cycles : 4 * cycles], z).astype(BF16)
        to_mate_sib.start()
        for q in range(chunks):
            to_next(q).wait_recv()
        w = meet(jnp.concatenate([leg_p[1, mate_z], legx[3]], axis=0), 1)
        harm_x[1] = (at_z(x[cycles : 2 * cycles], z) + at_z(w[cycles : 2 * cycles], mate_z)).astype(BF16)
        to_sib_x.start()
        harm_x[0] = (at_z(x[0:cycles], z) + at_z(w[0:cycles], mate_z)).astype(BF16)
        harm_r[4] = jnp.zeros((cycles, span), BF16)
        harm_r[5] = jnp.zeros((cycles, span), BF16)

    for zz in range(depth):
        for q in range(chunks):

            @pl.when((z < depth - 1) & (zz <= z))
            def _():
                to_up(zz, q).wait_send()

            @pl.when((z > 0) & (zz >= z))
            def _():
                to_down(zz, q).wait_send()

    for q in range(chunks):
        to_cross(q).wait_send()
    for k in range(far):
        for lane in range(2):
            leg_far(lane, k).wait_send()
    leg_sib.wait_send()
    leg_zsib.wait_send()
    leg_turn.wait_send()

    @pl.when(outer)
    def _():
        for q in range(chunks):
            to_next(q).wait_send()
        leg_quad.wait_send()

    @pl.when(inner)
    def _():
        to_mate.wait_send()
        to_mate_sib.wait_send()

    rows_cycle, rows_s = split_index(iota((rows_out, cycles), 0), REAL)
    repeat = jnp.where(rows_cycle == iota((rows_out, cycles), 1), 1.0, 0.0).astype(BF16)
    wide = group * span
    keep = split_index(iota((rows_out, wide), 0), REAL)[1] == split_index(iota((rows_out, wide), 1), REAL)[1]
    src_class, src_rest = split_index(iota((wide, 2 * subset), 0), span)
    src_z, src_c = split_index(src_rest, cols)
    src_dy, src_dc = split_index(src_class, 2)
    src_y = jnp.where(src_dy == 1, 1 - side, side)
    src_core = jnp.where(src_dc == 1, 1 - core, core)
    dst_part, dst_m = split_index(iota((wide, 2 * subset), 1), subset)
    hit = (split_index(src_c, REAL)[0] == dst_part) & (src_z * group + src_y * 2 + src_core == dst_m)
    select = jnp.where(hit, 1.0, 0.0).astype(BF16)

    to_sib_x.wait()

    @pl.when(outer)
    def _():
        to_mate.wait_recv()
        to_mate_sib.wait_recv()

    to_sib.wait()
    to_partner.wait()
    to_diag.wait()
    near = harm_x[0] + harm_r[1] + harm_r[4]
    away = harm_r[3] + harm_r[2] + harm_r[5]
    everything = jnp.concatenate([own, harm_r[0], near, away], axis=1)
    spread = jnp.dot(repeat, everything, preferred_element_type=F32)
    picked = jnp.where(keep, spread, 0.0).astype(BF16)
    out_ref[...] = jnp.dot(picked, select, preferred_element_type=F32).astype(BF16)


def synthesis_kernel(tiles, scale, h_v, table, out_ref, buf, sem):
    tile = out_ref.shape[1] // tiles
    copies = []
    for t in range(tiles):
        cut = slice(t * tile, (t + 1) * tile)
        total = jnp.dot(h_v[...], table[:, cut], preferred_element_type=F32)
        buf[:, cut] = (total * scale).astype(BF16)
        copies.append(pltpu.make_async_copy(buf.at[:, cut], out_ref.at[:, cut], sem.at[t]))
        copies[-1].start()
    for c in copies:
        c.wait()


def body(n, m_list, coeff, blocks, legendre):
    per_device, cols, order_max = coeff.shape
    assert per_device == 1 and n % 8 == 0
    cycles, subset, _ = legendre.shape
    chunks = 3
    depth = n // 4
    far = depth - 2
    width = order_max // chunks
    span = depth * cols
    rows_in, rows_out = cycles * subset, cycles * REAL
    keep = functools.partial(pltpu.with_memory_space_constraint, memory_space=pltpu.HBM)
    vmem = pl.BlockSpec(memory_space=pltpu.VMEM)
    hbm = pl.BlockSpec(memory_space=pltpu.HBM)
    dma = pltpu.SemaphoreType.DMA
    harmonics, table = pl.pallas_call(
        functools.partial(harmonics_kernel, n, chunks),
        out_shape=(
            jax.ShapeDtypeStruct((rows_out, 2 * subset), BF16),
            jax.ShapeDtypeStruct((2 * subset, NPHI), BF16),
        ),
        in_specs=[hbm, hbm, hbm, hbm],
        out_specs=(vmem, vmem),
        scratch_shapes=[
            pltpu.SMEM((subset,), jnp.int32),
            pltpu.VMEM((cols, order_max), BF16),
            pltpu.VMEM((chunks, order_max, width), BF16),
            pltpu.VMEM((rows_in, order_max), BF16),
            pltpu.VMEM((3, depth, cycles, order_max), BF16),
            pltpu.VMEM((2 * depth + 2 * far, cycles, order_max), BF16),
            pltpu.VMEM((4, cycles, order_max), BF16),
            pltpu.VMEM((chunks, depth, cols, width), BF16),
            pltpu.VMEM((chunks, 2, cols, width), BF16),
            pltpu.VMEM((3, cycles, span), BF16),
            pltpu.VMEM((4, cycles, span), BF16),
            pltpu.VMEM((6, cycles, span), BF16),
            dma((chunks + 3,)),
            dma((chunks, depth)),
            dma((chunks, depth)),
            dma((chunks, depth)),
            dma((chunks,)),
            dma((chunks, 2)),
            dma((chunks,)),
            dma((2,)),
            dma((2,)),
            dma((2, far)),
            dma((2, far)),
            dma((2,)),
            dma((1,)),
            dma((2,)),
            dma((6,)),
            dma((6,)),
        ],
        compiler_params=pltpu.CompilerParams(collective_id=0, has_side_effects=True, vmem_limit_bytes=40 << 20),
        name="harmonics",
    )(keep(m_list), keep(coeff), keep(blocks), keep(legendre.reshape(rows_in, order_max)))
    tiles = 8
    sky = pl.pallas_call(
        functools.partial(synthesis_kernel, tiles, 1.0 / math.sqrt(subset)),
        out_shape=jax.ShapeDtypeStruct((rows_out, NPHI), BF16),
        in_specs=[vmem, vmem],
        out_specs=hbm,
        scratch_shapes=[
            pltpu.VMEM((rows_out, NPHI), BF16),
            dma((tiles,)),
        ],
        name="synthesis", compiler_params=pltpu.CompilerParams(vmem_limit_bytes=40 << 20),
    )(harmonics, table)
    return sky.reshape(cycles, REAL, NPHI)


def solution(mesh):
    spec = P(("groups", "mset"), None, None)
    return jax.shard_map(
        functools.partial(body, mesh.shape["mset"]),
        mesh=mesh,
        in_specs=(P(), spec, spec, spec),
        out_specs=spec,
        check_vma=False,
    )
```

```python
import functools
import math

import jax
import jax.numpy as jnp
from jax import lax
from jax.experimental import pallas as pl
from jax.experimental.pallas import tpu as pltpu
from jax.sharding import PartitionSpec as P

LL = 3072
REAL = 16
NPHI = 8192
LANES = 128
MESH = pl.DeviceIdType.MESH
F32 = jnp.float32
BF16 = jnp.bfloat16
CHUNKS = 3


def iota(shape, dim):
    return lax.broadcasted_iota(jnp.int32, shape, dim)


def split_index(x, size):
    if size & (size - 1) == 0:
        shift = size.bit_length() - 1
        return lax.shift_right_logical(x, jnp.int32(shift)), lax.bitwise_and(x, jnp.int32(size - 1))
    quotient = x // size
    return quotient, x - quotient * size


def fill_table(m_s, table):
    subset = m_s.shape[0]
    m_col = jnp.zeros((subset, LANES), jnp.int32)
    slot = iota((subset, LANES), 0)
    for i in range(subset):
        m_col = jnp.where(slot == i, m_s[i], m_col)
    lane = iota((subset, LANES), 1)
    fine = split_index(m_col * lane, NPHI)[1].astype(F32) * (2.0 * math.pi / NPHI)
    coarse = split_index(m_col * (lane * LANES), NPHI)[1].astype(F32) * (2.0 * math.pi / NPHI)
    fine_cos, fine_sin = jnp.cos(fine), jnp.sin(fine)
    coarse_cos, coarse_sin = jnp.cos(coarse), jnp.sin(coarse)
    for a in range(NPHI // LANES):
        c = coarse_cos[:, a : a + 1]
        s = coarse_sin[:, a : a + 1]
        table[0:subset, a * LANES : (a + 1) * LANES] = (c * fine_cos - s * fine_sin).astype(BF16)
        table[subset : 2 * subset, a * LANES : (a + 1) * LANES] = (-(s * fine_cos + c * fine_sin)).astype(BF16)


def harmonics_kernel(
    n, chunks, m_ref, coeff_ref, blocks_ref, leg_ref, out_ref, table_ref,
    m_s, coeff_v, blocks_v, leg_v, leg_p, legs, legx, gathered, crossed, harm_s, harm_x, harm_r,
    load_sem, recv_sem, up_sem, down_sem, end_send, cross_send, cross_recv, next_send,
    sib_sem, zsib_sem, far_send, far_recv, quad_sem, low_send, low_recv, turn_send, turn_recv, harm_send, harm_recv,
):
    subset = m_ref.shape[0]
    cols, order_max = coeff_ref.shape[1], coeff_ref.shape[2]
    width = order_max // chunks
    group = 4
    depth = n // group
    far = depth - 2
    rows_in = leg_ref.shape[0]
    rows_out = out_ref.shape[0]
    cycles = rows_in // subset
    span = depth * cols
    me = lax.axis_index("mset")
    core = lax.rem(me, 2)
    side = lax.rem(lax.div(me, 2), 2)
    z = lax.div(me, group)
    sibling = me + 1 - 2 * core
    partner = me + 2 - 4 * side
    diagonal = sibling + 2 - 4 * side
    odd = lax.rem(z, 2)
    mate_z = z + 1 - 2 * odd
    mate = me + group - 2 * group * odd
    mate_sib = sibling + group - 2 * group * odd
    upper = z >= depth // 2
    outer = jnp.where(upper, odd == 1, odd == 0)
    inner = jnp.logical_not(outer)
    pair_lo = z - odd

    def remote(src, dst, send_sem, recv_sem_, target):
        return pltpu.make_async_remote_copy(
            src_ref=src, dst_ref=dst, send_sem=send_sem, recv_sem=recv_sem_,
            device_id={"mset": target}, device_id_type=MESH,
        )

    def load_block(q):
        return pltpu.make_async_copy(
            blocks_ref.at[0, :, pl.ds(q * width, width)], blocks_v.at[q], load_sem.at[q]
        )

    m_load = pltpu.make_async_copy(m_ref, m_s, load_sem.at[chunks + 2])
    coeff_load = pltpu.make_async_copy(coeff_ref.at[0], coeff_v, load_sem.at[chunks])
    leg_load = pltpu.make_async_copy(leg_ref, leg_v, load_sem.at[chunks + 1])
    m_load.start()
    coeff_load.start()
    for q in range(chunks):
        load_block(q).start()
    leg_load.start()

    barrier = pltpu.get_barrier_semaphore()

    def greet(target):
        pl.semaphore_signal(barrier, inc=1, device_id={"mset": target}, device_id_type=MESH)

    greet(sibling)
    greet(partner)
    greet(diagonal)
    greet(mate_sib)

    @pl.when(z == 0)
    def _():
        greet(me + (depth - 1) * group)

    @pl.when(z > 0)
    def _():
        greet(me - group)

    @pl.when(z < depth - 1)
    def _():
        greet(me + group)

    def to_up(zz, q):
        piece = gathered.at[q, zz]
        return remote(piece, piece, up_sem.at[q, zz], recv_sem.at[q, zz], me + group)

    def to_down(zz, q):
        piece = gathered.at[q, zz]
        return remote(piece, piece, down_sem.at[q, zz], recv_sem.at[q, zz], me - group)

    def to_end(q):
        piece = gathered.at[q, depth - 1]
        return remote(piece, piece, end_send.at[q], recv_sem.at[q, depth - 1], me - (depth - 1) * group)

    def arrive(zz, q):
        piece = gathered.at[q, zz]
        remote(piece, piece, up_sem.at[q, 0], recv_sem.at[q, zz], sibling).wait_recv()

    def to_cross(q):
        return remote(gathered.at[q, z], crossed.at[q, 0], cross_send.at[q], cross_recv.at[q, 0], partner)

    def to_next(q):
        return remote(crossed.at[q, 0], crossed.at[q, 1], next_send.at[q], cross_recv.at[q, 1], mate)

    leg_sib = remote(leg_p.at[0], legs.at[pl.ds(depth, depth)], sib_sem.at[0], sib_sem.at[1], sibling)
    leg_zsib = remote(leg_p.at[2, z], legx.at[0], zsib_sem.at[0], zsib_sem.at[1], sibling)

    def far_z(k):
        return k + jnp.where(k >= pair_lo, 2, 0)

    def leg_far(lane, k):
        target = diagonal if lane else partner
        return remote(
            leg_p.at[1 + lane, far_z(k)], legs.at[2 * depth + lane * far + k],
            far_send.at[lane, k], far_recv.at[lane, k], target,
        )

    leg_quad = remote(leg_p.at[1, mate_z], legx.at[1], quad_sem.at[0], quad_sem.at[1], mate)
    turn_slot = jnp.where(outer, 0, 1)
    leg_turn = remote(
        leg_p.at[2, mate_z], legx.at[2 + turn_slot], turn_send.at[0], turn_recv.at[turn_slot],
        jnp.where(outer, mate_sib, sibling),
    )

    leg_low = remote(legs.at[1], legx.at[4], low_send.at[0], low_recv.at[0], mate)
    leg_low_sib = remote(leg_p.at[0, 1], legx.at[5], low_send.at[1], low_recv.at[1], mate_sib)

    m_load.wait()
    order = LL - m_s[me]
    coeff_load.wait()
    masked = jnp.where(iota((cols, order_max), 1) < order, coeff_v[...].astype(F32), 0.0).astype(BF16)

    def filter_chunk(q):
        load_block(q).wait()
        product = jnp.dot(masked, blocks_v[q], preferred_element_type=F32)
        valid = iota((cols, width), 1) + q * width < order
        gathered[q, z] = jnp.where(valid, product, 0.0).astype(BF16)

        if q == 0:
            peers = 4 + jnp.where(z > 0, 1, 0) + jnp.where(z < depth - 1, 1, 1)
            pl.semaphore_wait(barrier, peers)

        @pl.when(z == depth - 1)
        def _():
            to_end(q).start()

        @pl.when(z < depth - 1)
        def _():
            to_up(z, q).start()

        @pl.when(z > 1)
        def _():
            to_down(z, q).start()

        to_cross(q).start()

    for q in range(chunks):
        filter_chunk(q)

    rows_all = group * depth * cycles
    row_class, row_rest = split_index(iota((rows_all, rows_in), 0), depth * cycles)
    row_z, row_cycle = split_index(row_rest, cycles)
    row_dy, row_dc = split_index(row_class, 2)
    row_y = jnp.where(row_dy == 1, 1 - side, side)
    row_c = jnp.where(row_dc == 1, 1 - core, core)
    wanted = row_cycle * subset + row_z * group + row_y * 2 + row_c
    permute = jnp.where(iota((rows_all, rows_in), 1) == wanted, 1.0, 0.0).astype(BF16)
    leg_load.wait()
    for q in range(chunks):
        cut = slice(q * width, (q + 1) * width)
        moved = jnp.dot(permute, leg_v[:, cut], preferred_element_type=F32).astype(BF16)
        moved = moved.reshape(group, depth, cycles, width)
        legs[0:depth, :, cut] = moved[0]
        leg_p[:, :, :, cut] = moved[1:]

    for k in range(far):
        for lane in range(2):
            leg_far(lane, k).start()

    @pl.when(outer)
    def _():
        leg_quad.start()

    leg_turn.start()

    @pl.when(z == 0)
    def _():
        leg_low.start()
        leg_low_sib.start()

    leg_sib.start()
    leg_zsib.start()

    fill_table(m_s, table_ref)

    def below(d, q):
        arrive(z - d, q)

        @pl.when(z < depth - 1)
        def _():
            to_up(z - d, q).start()

    def above(d, q):
        arrive(z + d, q)
        if d < depth - 2:

            @pl.when(z > 0)
            def _():
                to_down(z + d, q).start()

    def cross_arrive(q):
        to_cross(q).wait_recv()

        @pl.when(outer)
        def _():
            to_next(q).start()

    def relay(d, q):
        pl.when(z >= d)(functools.partial(below, d, q))
        pl.when((z <= depth - 1 - d) & (z > (0 if d == 1 else -1)))(functools.partial(above, d, q))

    for d in range(1, depth - 1):
        for q in range(chunks):
            relay(d, q)
            if d == 1:
                cross_arrive(q)

    lane_z = split_index(iota((cycles, span), 1), cols)[0]

    def at_z(x, zz):
        return jnp.where(lane_z == zz, x, 0.0)

    contract_last = (((1,), (1,)), ((), ()))

    def meet(rows, block):
        total = jnp.zeros((rows.shape[0], span), F32)
        for q in range(chunks):
            f = block(q)
            total += lax.dot_general(
                rows[:, q * width : (q + 1) * width], jnp.concatenate([f] * depth, axis=0),
                contract_last, preferred_element_type=F32,
            )
        return total

    def harm_copy(src, slot, target):
        dst = harm_r.at[slot] if slot < 4 else harm_r.at[pl.ds(2 * slot - 4, 2)]
        return remote(src, dst, harm_send.at[slot], harm_recv.at[slot], target)

    to_sib = harm_copy(harm_s.at[0], 0, sibling)
    to_partner = harm_copy(harm_s.at[1], 1, partner)
    to_diag = harm_copy(harm_s.at[2], 2, diagonal)
    to_sib_x = harm_copy(harm_x.at[1], 3, sibling)
    to_mate = harm_copy(harm_x.at[pl.ds(2, 2)], 4, mate)
    to_mate_sib = harm_copy(harm_x.at[pl.ds(4, 2)], 5, mate_sib)

    leg_zsib.wait_recv()

    @pl.when(outer)
    def _():
        x = meet(jnp.concatenate([leg_p[1, z], legx[0]], axis=0), lambda q: crossed[q, 0])
        harm_x[0] = at_z(x[0:cycles], z).astype(BF16)
        harm_x[1] = at_z(x[cycles : 2 * cycles], z).astype(BF16)
        to_sib_x.start()

    @pl.when(inner)
    def _():
        leg_quad.wait_recv()
        remote(leg_p.at[2, mate_z], legx.at[2], turn_send.at[0], turn_recv.at[0], sibling).wait_recv()
        x = meet(jnp.concatenate([leg_p[1, z], legx[0], legx[1], legx[2]], axis=0), lambda q: crossed[q, 0])
        harm_x[0] = at_z(x[0:cycles], z).astype(BF16)
        harm_x[1] = at_z(x[cycles : 2 * cycles], z).astype(BF16)
        harm_x[2] = at_z(x[2 * cycles : 3 * cycles], z).astype(BF16)
        harm_x[4] = at_z(x[3 * cycles : 4 * cycles], z).astype(BF16)
        harm_x[3] = jnp.zeros((cycles, span), BF16)
        harm_x[5] = jnp.zeros((cycles, span), BF16)
        harm_r[4:8] = jnp.zeros((4, cycles, span), BF16)

    @pl.when(z == 1)
    def _():
        leg_low.wait_recv()
        leg_low_sib.wait_recv()
        x = meet(jnp.concatenate([legx[4], legx[5]], axis=0), lambda q: gathered[q, z])
        harm_x[3] = at_z(x[0:cycles], z).astype(BF16)
        harm_x[5] = at_z(x[cycles : 2 * cycles], z).astype(BF16)

    @pl.when(inner)
    def _():
        to_mate.start()
        to_mate_sib.start()

    @pl.when(z == 0)
    def _():
        gathered[:, 1] = jnp.zeros((chunks, cols, width), BF16)

    leg_sib.wait_recv()
    total_rows = (2 * depth + 2 * far) * cycles
    cross = jnp.zeros((total_rows, span), F32)
    for q in range(chunks):
        relay(depth - 1, q)
        if q == 0:
            for k in range(far):
                for lane in range(2):
                    leg_far(lane, k).wait_recv()
        cross += lax.dot_general(
            legs[:, :, q * width : (q + 1) * width].reshape(total_rows, width),
            gathered[q].reshape(span, width),
            contract_last, preferred_element_type=F32,
        )

    def collect(first, zs):
        out = jnp.zeros((cycles, span), F32)
        for k, zz in enumerate(zs):
            out += at_z(cross[(first + k) * cycles : (first + k + 1) * cycles], zz)
        return out.astype(BF16)

    far_list = [far_z(k) for k in range(far)]
    harm_s[1] = collect(2 * depth, far_list)
    to_partner.start()
    harm_s[2] = collect(2 * depth + far, far_list)
    to_diag.start()
    harm_s[0] = collect(depth, range(depth))
    to_sib.start()
    own = collect(0, range(depth))

    @pl.when(inner)
    def _():
        for q in range(chunks):
            to_next(q).wait_recv()
        remote(leg_p.at[2, mate_z], legx.at[3], turn_send.at[0], turn_recv.at[1], sibling).wait_recv()
        w = meet(jnp.concatenate([leg_p[1, mate_z], legx[3]], axis=0), lambda q: crossed[q, 1])
        harm_x[1] = harm_x[1] + at_z(w[cycles : 2 * cycles], mate_z).astype(BF16)
        to_sib_x.start()
        harm_x[0] = harm_x[0] + at_z(w[0:cycles], mate_z).astype(BF16)

    for zz in range(depth):
        for q in range(chunks):

            @pl.when((z < depth - 1) & (zz <= z))
            def _():
                to_up(zz, q).wait_send()

            @pl.when((z > (1 if zz in (1, depth - 1) else 0)) & (zz >= z))
            def _():
                to_down(zz, q).wait_send()

    for q in range(chunks):
        to_cross(q).wait_send()

        @pl.when(z == depth - 1)
        def _():
            to_end(q).wait_send()

    for k in range(far):
        for lane in range(2):
            leg_far(lane, k).wait_send()
    leg_sib.wait_send()
    leg_zsib.wait_send()
    leg_turn.wait_send()

    @pl.when(outer)
    def _():
        for q in range(chunks):
            to_next(q).wait_send()
        leg_quad.wait_send()

    @pl.when(z == 0)
    def _():
        leg_low.wait_send()
        leg_low_sib.wait_send()

    @pl.when(inner)
    def _():
        to_mate.wait_send()
        to_mate_sib.wait_send()

    rows_cycle, rows_s = split_index(iota((rows_out, cycles), 0), REAL)
    repeat = jnp.where(rows_cycle == iota((rows_out, cycles), 1), 1.0, 0.0).astype(BF16)
    wide = group * span
    keep = split_index(iota((rows_out, wide), 0), REAL)[1] == split_index(iota((rows_out, wide), 1), REAL)[1]
    src_class, src_rest = split_index(iota((wide, 2 * subset), 0), span)
    src_z, src_c = split_index(src_rest, cols)
    src_dy, src_dc = split_index(src_class, 2)
    src_y = jnp.where(src_dy == 1, 1 - side, side)
    src_core = jnp.where(src_dc == 1, 1 - core, core)
    dst_part, dst_m = split_index(iota((wide, 2 * subset), 1), subset)
    hit = (split_index(src_c, REAL)[0] == dst_part) & (src_z * group + src_y * 2 + src_core == dst_m)
    select = jnp.where(hit, 1.0, 0.0).astype(BF16)

    to_sib_x.wait()

    @pl.when(outer)
    def _():
        to_mate.wait_recv()
        to_mate_sib.wait_recv()

    to_sib.wait()
    to_partner.wait()
    to_diag.wait()
    near = harm_x[0] + harm_r[1] + harm_r[4]
    away = harm_r[3] + harm_r[2] + harm_r[6]
    everything = jnp.concatenate([own + harm_r[5], harm_r[0] + harm_r[7], near, away], axis=1)
    spread = jnp.dot(repeat, everything, preferred_element_type=F32)
    picked = jnp.where(keep, spread, 0.0).astype(BF16)
    out_ref[...] = jnp.dot(picked, select, preferred_element_type=F32).astype(BF16)


def synthesis_kernel(tiles, scale, h_v, table, out_ref, buf, sem):
    tile = out_ref.shape[1] // tiles
    copies = []
    for t in range(tiles):
        cut = slice(t * tile, (t + 1) * tile)
        total = jnp.dot(h_v[...], table[:, cut], preferred_element_type=F32)
        buf[:, cut] = (total * scale).astype(BF16)
        copies.append(pltpu.make_async_copy(buf.at[:, cut], out_ref.at[:, cut], sem.at[t]))
        copies[-1].start()
    for c in copies:
        c.wait()


def body(n, m_list, coeff, blocks, legendre):
    per_device, cols, order_max = coeff.shape
    assert per_device == 1 and n % 16 == 0 and order_max % (CHUNKS * LANES) == 0
    cycles, subset, _ = legendre.shape
    chunks = CHUNKS
    depth = n // 4
    far = depth - 2
    width = order_max // chunks
    span = depth * cols
    rows_in, rows_out = cycles * subset, cycles * REAL
    keep = functools.partial(pltpu.with_memory_space_constraint, memory_space=pltpu.HBM)
    vmem = pl.BlockSpec(memory_space=pltpu.VMEM)
    hbm = pl.BlockSpec(memory_space=pltpu.HBM)
    dma = pltpu.SemaphoreType.DMA
    harmonics, table = pl.pallas_call(
        functools.partial(harmonics_kernel, n, chunks),
        out_shape=(
            jax.ShapeDtypeStruct((rows_out, 2 * subset), BF16),
            jax.ShapeDtypeStruct((2 * subset, NPHI), BF16),
        ),
        in_specs=[hbm, hbm, hbm, hbm],
        out_specs=(vmem, vmem),
        scratch_shapes=[
            pltpu.SMEM((subset,), jnp.int32),
            pltpu.VMEM((cols, order_max), BF16),
            pltpu.VMEM((chunks, order_max, width), BF16),
            pltpu.VMEM((rows_in, order_max), BF16),
            pltpu.VMEM((3, depth, cycles, order_max), BF16),
            pltpu.VMEM((2 * depth + 2 * far, cycles, order_max), BF16),
            pltpu.VMEM((6, cycles, order_max), BF16),
            pltpu.VMEM((chunks, depth, cols, width), BF16),
            pltpu.VMEM((chunks, 2, cols, width), BF16),
            pltpu.VMEM((3, cycles, span), BF16),
            pltpu.VMEM((6, cycles, span), BF16),
            pltpu.VMEM((8, cycles, span), BF16),
            dma((chunks + 3,)),
            dma((chunks, depth)),
            dma((chunks, depth)),
            dma((chunks, depth)),
            dma((chunks,)),
            dma((chunks,)),
            dma((chunks, 2)),
            dma((chunks,)),
            dma((2,)),
            dma((2,)),
            dma((2, far)),
            dma((2, far)),
            dma((2,)),
            dma((2,)),
            dma((2,)),
            dma((1,)),
            dma((2,)),
            dma((6,)),
            dma((6,)),
        ],
        compiler_params=pltpu.CompilerParams(collective_id=0, has_side_effects=True, vmem_limit_bytes=40 << 20),
        name="harmonics",
    )(keep(m_list), keep(coeff), keep(blocks), keep(legendre.reshape(rows_in, order_max)))
    tiles = 8
    sky = pl.pallas_call(
        functools.partial(synthesis_kernel, tiles, 1.0 / math.sqrt(subset)),
        out_shape=jax.ShapeDtypeStruct((rows_out, NPHI), BF16),
        in_specs=[vmem, vmem],
        out_specs=hbm,
        scratch_shapes=[
            pltpu.VMEM((rows_out, NPHI), BF16),
            dma((tiles,)),
        ],
        name="synthesis", compiler_params=pltpu.CompilerParams(vmem_limit_bytes=40 << 20),
    )(harmonics, table)
    return sky.reshape(cycles, REAL, NPHI)


def solution(mesh):
    spec = P(("groups", "mset"), None, None)
    return jax.shard_map(
        functools.partial(body, mesh.shape["mset"]),
        mesh=mesh,
        in_specs=(P(), spec, spec, spec),
        out_specs=spec,
        check_vma=False,
    )
```

```python
import functools
import math

import jax
import jax.numpy as jnp
from jax import lax
from jax.experimental import pallas as pl
from jax.experimental.pallas import tpu as pltpu
from jax.sharding import PartitionSpec as P

LL = 3072
REAL = 16
NPHI = 8192
LANES = 128
MESH = pl.DeviceIdType.MESH
F32 = jnp.float32
BF16 = jnp.bfloat16
CHUNKS = 3


def iota(shape, dim):
    return lax.broadcasted_iota(jnp.int32, shape, dim)


def split_index(x, size):
    if size & (size - 1) == 0:
        shift = size.bit_length() - 1
        return lax.shift_right_logical(x, jnp.int32(shift)), lax.bitwise_and(x, jnp.int32(size - 1))
    quotient = x // size
    return quotient, x - quotient * size


def fill_table(m_s, table):
    subset = m_s.shape[0]
    m_col = jnp.zeros((subset, LANES), jnp.int32)
    slot = iota((subset, LANES), 0)
    for i in range(subset):
        m_col = jnp.where(slot == i, m_s[i], m_col)
    lane = iota((subset, LANES), 1)
    fine = split_index(m_col * lane, NPHI)[1].astype(F32) * (2.0 * math.pi / NPHI)
    coarse = split_index(m_col * (lane * LANES), NPHI)[1].astype(F32) * (2.0 * math.pi / NPHI)
    fine_cos, fine_sin = jnp.cos(fine), jnp.sin(fine)
    coarse_cos, coarse_sin = jnp.cos(coarse), jnp.sin(coarse)
    for a in range(NPHI // LANES):
        c = coarse_cos[:, a : a + 1]
        s = coarse_sin[:, a : a + 1]
        table[0:subset, a * LANES : (a + 1) * LANES] = (c * fine_cos - s * fine_sin).astype(BF16)
        table[subset : 2 * subset, a * LANES : (a + 1) * LANES] = (-(s * fine_cos + c * fine_sin)).astype(BF16)


def harmonics_kernel(
    n, chunks, m_ref, coeff_ref, blocks_ref, leg_ref, out_ref, table_ref,
    m_s, coeff_v, blocks_v, leg_v, leg_p, legs, legx, gathered, crossed, harm_s, harm_x, harm_r,
    load_sem, recv_sem, up_sem, down_sem, end_send, cross_send, cross_recv, next_send,
    sib_sem, zsib_sem, far_send, far_recv, quad_sem, low_send, low_recv, turn_send, turn_recv, harm_send, harm_recv,
):
    subset = m_ref.shape[0]
    cols, order_max = coeff_ref.shape[1], coeff_ref.shape[2]
    width = order_max // chunks
    group = 4
    depth = n // group
    far = depth - 2
    rows_in = leg_ref.shape[0]
    rows_out = out_ref.shape[0]
    cycles = rows_in // subset
    span = depth * cols
    me = lax.axis_index("mset")
    core = lax.rem(me, 2)
    side = lax.rem(lax.div(me, 2), 2)
    z = lax.div(me, group)
    sibling = me + 1 - 2 * core
    partner = me + 2 - 4 * side
    diagonal = sibling + 2 - 4 * side
    odd = lax.rem(z, 2)
    mate_z = z + 1 - 2 * odd
    mate = me + group - 2 * group * odd
    mate_sib = sibling + group - 2 * group * odd
    upper = z >= depth // 2
    outer = jnp.where(upper, odd == 1, odd == 0)
    inner = jnp.logical_not(outer)
    pair_lo = z - odd

    def remote(src, dst, send_sem, recv_sem_, target):
        return pltpu.make_async_remote_copy(
            src_ref=src, dst_ref=dst, send_sem=send_sem, recv_sem=recv_sem_,
            device_id={"mset": target}, device_id_type=MESH,
        )

    def load_block(q):
        return pltpu.make_async_copy(
            blocks_ref.at[0, :, pl.ds(q * width, width)], blocks_v.at[q], load_sem.at[q]
        )

    m_load = pltpu.make_async_copy(m_ref, m_s, load_sem.at[chunks + 2])
    coeff_load = pltpu.make_async_copy(coeff_ref.at[0], coeff_v, load_sem.at[chunks])
    leg_load = pltpu.make_async_copy(leg_ref, leg_v, load_sem.at[chunks + 1])
    m_load.start()
    coeff_load.start()
    for q in range(chunks):
        load_block(q).start()
    leg_load.start()

    barrier = pltpu.get_barrier_semaphore()

    def greet(target):
        pl.semaphore_signal(barrier, inc=1, device_id={"mset": target}, device_id_type=MESH)

    greet(sibling)
    greet(partner)
    greet(diagonal)
    greet(mate_sib)

    @pl.when(z == 0)
    def _():
        greet(me + (depth - 1) * group)

    @pl.when(z > 0)
    def _():
        greet(me - group)

    @pl.when(z < depth - 1)
    def _():
        greet(me + group)

    def to_up(zz, q):
        piece = gathered.at[q, zz]
        return remote(piece, piece, up_sem.at[q, zz], recv_sem.at[q, zz], me + group)

    def to_down(zz, q):
        piece = gathered.at[q, zz]
        return remote(piece, piece, down_sem.at[q, zz], recv_sem.at[q, zz], me - group)

    def to_end(q):
        piece = gathered.at[q, depth - 1]
        return remote(piece, piece, end_send.at[q], recv_sem.at[q, depth - 1], me - (depth - 1) * group)

    def arrive(zz, q):
        piece = gathered.at[q, zz]
        remote(piece, piece, up_sem.at[q, 0], recv_sem.at[q, zz], sibling).wait_recv()

    def to_cross(q):
        return remote(gathered.at[q, z], crossed.at[q, 0], cross_send.at[q], cross_recv.at[q, 0], partner)

    def to_next(q):
        return remote(crossed.at[q, 0], crossed.at[q, 1], next_send.at[q], cross_recv.at[q, 1], mate)

    leg_sib = remote(leg_p.at[0], legs.at[pl.ds(depth, depth)], sib_sem.at[0], sib_sem.at[1], sibling)
    leg_zsib = remote(leg_p.at[2, z], legx.at[0], zsib_sem.at[0], zsib_sem.at[1], sibling)

    def far_z(k):
        return k + jnp.where(k >= pair_lo, 2, 0)

    def leg_far(lane, k):
        target = diagonal if lane else partner
        return remote(
            leg_p.at[1 + lane, far_z(k)], legs.at[2 * depth + lane * far + k],
            far_send.at[lane, k], far_recv.at[lane, k], target,
        )

    leg_quad = remote(leg_p.at[1, mate_z], legx.at[1], quad_sem.at[0], quad_sem.at[1], mate)
    turn_slot = jnp.where(outer, 0, 1)
    leg_turn = remote(
        leg_p.at[2, mate_z], legx.at[2 + turn_slot], turn_send.at[0], turn_recv.at[turn_slot],
        jnp.where(outer, mate_sib, sibling),
    )

    leg_low = remote(legs.at[1], legx.at[4], low_send.at[0], low_recv.at[0], mate)
    leg_low_sib = remote(leg_p.at[0, 1], legx.at[5], low_send.at[1], low_recv.at[1], mate_sib)

    m_load.wait()
    order = LL - m_s[me]
    coeff_load.wait()
    masked = jnp.where(iota((cols, order_max), 1) < order, coeff_v[...].astype(F32), 0.0).astype(BF16)

    def filter_chunk(q):
        load_block(q).wait()
        product = jnp.dot(masked, blocks_v[q], preferred_element_type=F32)
        valid = iota((cols, width), 1) + q * width < order
        gathered[q, z] = jnp.where(valid, product, 0.0).astype(BF16)

        if q == 0:
            peers = 4 + jnp.where(z > 0, 1, 0) + jnp.where(z < depth - 1, 1, 1)
            pl.semaphore_wait(barrier, peers)

        @pl.when(z == depth - 1)
        def _():
            to_end(q).start()

        @pl.when(z < depth - 1)
        def _():
            to_up(z, q).start()

        @pl.when(z > 1)
        def _():
            to_down(z, q).start()

        to_cross(q).start()

    for q in range(chunks):
        filter_chunk(q)


    rows_all = group * depth * cycles
    row_class, row_rest = split_index(iota((rows_all, rows_in), 0), depth * cycles)
    row_z, row_cycle = split_index(row_rest, cycles)
    row_dy, row_dc = split_index(row_class, 2)
    row_y = jnp.where(row_dy == 1, 1 - side, side)
    row_c = jnp.where(row_dc == 1, 1 - core, core)
    wanted = row_cycle * subset + row_z * group + row_y * 2 + row_c
    permute = jnp.where(iota((rows_all, rows_in), 1) == wanted, 1.0, 0.0).astype(BF16)
    leg_load.wait()
    for q in range(chunks):
        cut = slice(q * width, (q + 1) * width)
        moved = jnp.dot(permute, leg_v[:, cut], preferred_element_type=F32).astype(BF16)
        moved = moved.reshape(group, depth, cycles, width)
        legs[0:depth, :, cut] = moved[0]
        leg_p[:, :, :, cut] = moved[1:]

    for k in range(far):
        for lane in range(2):
            leg_far(lane, k).start()

    @pl.when(outer)
    def _():
        leg_quad.start()

    leg_turn.start()

    @pl.when(z == 0)
    def _():
        leg_low.start()
        leg_low_sib.start()

    leg_sib.start()
    leg_zsib.start()

    fill_table(m_s, table_ref)

    def below(d, q):
        arrive(z - d, q)
        to_up(z - d, q).start()

    def above(d, q):
        arrive(z + d, q)
        to_down(z + d, q).start()

    def take(zz, q):
        arrive(zz, q)

    for d in range(1, depth - 1):
        for q in range(chunks):
            pl.when((z >= d) & (z < depth - 1))(functools.partial(below, d, q))

    @pl.when(outer)
    def _():
        for q in range(chunks):
            to_cross(q).wait_recv()
            to_next(q).start()

    for d in range(1, depth - 1):
        for q in range(chunks):
            pl.when((z <= depth - 1 - d) & (z > (1 if d == depth - 2 else 0)))(functools.partial(above, d, q))

    lane_z = split_index(iota((cycles, span), 1), cols)[0]

    def at_z(x, zz):
        return jnp.where(lane_z == zz, x, 0.0)

    contract_last = (((1,), (1,)), ((), ()))

    def meet(rows, block):
        total = jnp.zeros((rows.shape[0], span), F32)
        for q in range(chunks):
            f = block(q)
            total += lax.dot_general(
                rows[:, q * width : (q + 1) * width], jnp.concatenate([f] * depth, axis=0),
                contract_last, preferred_element_type=F32,
            )
        return total

    def harm_copy(src, slot, target):
        dst = harm_r.at[slot] if slot < 4 else harm_r.at[pl.ds(2 * slot - 4, 2)]
        return remote(src, dst, harm_send.at[slot], harm_recv.at[slot], target)

    to_sib = harm_copy(harm_s.at[0], 0, sibling)
    to_partner = harm_copy(harm_s.at[1], 1, partner)
    to_diag = harm_copy(harm_s.at[2], 2, diagonal)
    to_sib_x = harm_copy(harm_x.at[1], 3, sibling)
    to_mate = harm_copy(harm_x.at[pl.ds(2, 2)], 4, mate)
    to_mate_sib = harm_copy(harm_x.at[pl.ds(4, 2)], 5, mate_sib)

    leg_zsib.wait_recv()

    @pl.when(outer)
    def _():
        x = meet(jnp.concatenate([leg_p[1, z], legx[0]], axis=0), lambda q: crossed[q, 0])
        harm_x[0] = at_z(x[0:cycles], z).astype(BF16)
        harm_x[1] = at_z(x[cycles : 2 * cycles], z).astype(BF16)
        to_sib_x.start()

    @pl.when(inner)
    def _():
        for q in range(chunks):
            to_cross(q).wait_recv()
        leg_quad.wait_recv()
        remote(leg_p.at[2, mate_z], legx.at[2], turn_send.at[0], turn_recv.at[0], sibling).wait_recv()
        x = meet(jnp.concatenate([leg_p[1, z], legx[0], legx[1], legx[2]], axis=0), lambda q: crossed[q, 0])
        harm_x[0] = at_z(x[0:cycles], z).astype(BF16)
        harm_x[1] = at_z(x[cycles : 2 * cycles], z).astype(BF16)
        harm_x[2] = at_z(x[2 * cycles : 3 * cycles], z).astype(BF16)
        harm_x[4] = at_z(x[3 * cycles : 4 * cycles], z).astype(BF16)
        harm_x[3] = jnp.zeros((cycles, span), BF16)
        harm_x[5] = jnp.zeros((cycles, span), BF16)
        harm_r[4:8] = jnp.zeros((4, cycles, span), BF16)

    @pl.when(z == 1)
    def _():
        leg_low.wait_recv()
        leg_low_sib.wait_recv()
        x = meet(jnp.concatenate([legx[4], legx[5]], axis=0), lambda q: gathered[q, z])
        harm_x[3] = at_z(x[0:cycles], z).astype(BF16)
        harm_x[5] = at_z(x[cycles : 2 * cycles], z).astype(BF16)

    @pl.when(inner)
    def _():
        to_mate.start()
        to_mate_sib.start()

    @pl.when(z == 0)
    def _():
        gathered[:, 1] = jnp.zeros((chunks, cols, width), BF16)

    leg_sib.wait_recv()
    total_rows = (2 * depth + 2 * far) * cycles
    cross = jnp.zeros((total_rows, span), F32)
    for q in range(chunks):
        pl.when(z == 1)(functools.partial(take, depth - 1, q))
        for d in range(1, depth):
            if d > 1:
                pl.when(z == 0)(functools.partial(take, d, q))
            pl.when(z == depth - 1)(functools.partial(take, depth - 1 - d, q))
        if q == 0:
            for k in range(far):
                for lane in range(2):
                    leg_far(lane, k).wait_recv()
        cross += lax.dot_general(
            legs[:, :, q * width : (q + 1) * width].reshape(total_rows, width),
            gathered[q].reshape(span, width),
            contract_last, preferred_element_type=F32,
        )

    def collect(first, zs):
        out = jnp.zeros((cycles, span), F32)
        for k, zz in enumerate(zs):
            out += at_z(cross[(first + k) * cycles : (first + k + 1) * cycles], zz)
        return out.astype(BF16)

    far_list = [far_z(k) for k in range(far)]
    harm_s[1] = collect(2 * depth, far_list)
    to_partner.start()
    harm_s[2] = collect(2 * depth + far, far_list)
    to_diag.start()
    harm_s[0] = collect(depth, range(depth))
    to_sib.start()
    own = collect(0, range(depth))

    @pl.when(inner)
    def _():
        for q in range(chunks):
            to_next(q).wait_recv()
        remote(leg_p.at[2, mate_z], legx.at[3], turn_send.at[0], turn_recv.at[1], sibling).wait_recv()
        w = meet(jnp.concatenate([leg_p[1, mate_z], legx[3]], axis=0), lambda q: crossed[q, 1])
        harm_x[1] = harm_x[1] + at_z(w[cycles : 2 * cycles], mate_z).astype(BF16)
        to_sib_x.start()
        harm_x[0] = harm_x[0] + at_z(w[0:cycles], mate_z).astype(BF16)

    for zz in range(depth):
        for q in range(chunks):

            @pl.when((z < depth - 1) & (zz <= z))
            def _():
                to_up(zz, q).wait_send()

            @pl.when((z > (1 if zz in (1, depth - 1) else 0)) & (zz >= z))
            def _():
                to_down(zz, q).wait_send()

    for q in range(chunks):
        to_cross(q).wait_send()

        @pl.when(z == depth - 1)
        def _():
            to_end(q).wait_send()

    for k in range(far):
        for lane in range(2):
            leg_far(lane, k).wait_send()
    leg_sib.wait_send()
    leg_zsib.wait_send()
    leg_turn.wait_send()

    @pl.when(outer)
    def _():
        for q in range(chunks):
            to_next(q).wait_send()
        leg_quad.wait_send()

    @pl.when(z == 0)
    def _():
        leg_low.wait_send()
        leg_low_sib.wait_send()

    @pl.when(inner)
    def _():
        to_mate.wait_send()
        to_mate_sib.wait_send()

    rows_cycle, rows_s = split_index(iota((rows_out, cycles), 0), REAL)
    repeat = jnp.where(rows_cycle == iota((rows_out, cycles), 1), 1.0, 0.0).astype(BF16)
    wide = group * span
    keep = split_index(iota((rows_out, wide), 0), REAL)[1] == split_index(iota((rows_out, wide), 1), REAL)[1]
    src_class, src_rest = split_index(iota((wide, 2 * subset), 0), span)
    src_z, src_c = split_index(src_rest, cols)
    src_dy, src_dc = split_index(src_class, 2)
    src_y = jnp.where(src_dy == 1, 1 - side, side)
    src_core = jnp.where(src_dc == 1, 1 - core, core)
    dst_part, dst_m = split_index(iota((wide, 2 * subset), 1), subset)
    hit = (split_index(src_c, REAL)[0] == dst_part) & (src_z * group + src_y * 2 + src_core == dst_m)
    select = jnp.where(hit, 1.0, 0.0).astype(BF16)

    to_sib_x.wait()

    @pl.when(outer)
    def _():
        to_mate.wait_recv()
        to_mate_sib.wait_recv()

    to_sib.wait()
    to_partner.wait()
    to_diag.wait()
    near = harm_x[0] + harm_r[1] + harm_r[4]
    away = harm_r[3] + harm_r[2] + harm_r[6]
    everything = jnp.concatenate([own + harm_r[5], harm_r[0] + harm_r[7], near, away], axis=1)
    spread = jnp.dot(repeat, everything, preferred_element_type=F32)
    picked = jnp.where(keep, spread, 0.0).astype(BF16)
    out_ref[...] = jnp.dot(picked, select, preferred_element_type=F32).astype(BF16)


def synthesis_kernel(tiles, scale, h_v, table, out_ref, buf, sem):
    tile = out_ref.shape[1] // tiles
    copies = []
    for t in range(tiles):
        cut = slice(t * tile, (t + 1) * tile)
        total = jnp.dot(h_v[...], table[:, cut], preferred_element_type=F32)
        buf[:, cut] = (total * scale).astype(BF16)
        copies.append(pltpu.make_async_copy(buf.at[:, cut], out_ref.at[:, cut], sem.at[t]))
        copies[-1].start()
    for c in copies:
        c.wait()


def body(n, m_list, coeff, blocks, legendre):
    per_device, cols, order_max = coeff.shape
    assert per_device == 1 and n % 16 == 0 and order_max % (CHUNKS * LANES) == 0
    cycles, subset, _ = legendre.shape
    chunks = CHUNKS
    depth = n // 4
    far = depth - 2
    width = order_max // chunks
    span = depth * cols
    rows_in, rows_out = cycles * subset, cycles * REAL
    keep = functools.partial(pltpu.with_memory_space_constraint, memory_space=pltpu.HBM)
    vmem = pl.BlockSpec(memory_space=pltpu.VMEM)
    hbm = pl.BlockSpec(memory_space=pltpu.HBM)
    dma = pltpu.SemaphoreType.DMA
    harmonics, table = pl.pallas_call(
        functools.partial(harmonics_kernel, n, chunks),
        out_shape=(
            jax.ShapeDtypeStruct((rows_out, 2 * subset), BF16),
            jax.ShapeDtypeStruct((2 * subset, NPHI), BF16),
        ),
        in_specs=[hbm, hbm, hbm, hbm],
        out_specs=(vmem, vmem),
        scratch_shapes=[
            pltpu.SMEM((subset,), jnp.int32),
            pltpu.VMEM((cols, order_max), BF16),
            pltpu.VMEM((chunks, order_max, width), BF16),
            pltpu.VMEM((rows_in, order_max), BF16),
            pltpu.VMEM((3, depth, cycles, order_max), BF16),
            pltpu.VMEM((2 * depth + 2 * far, cycles, order_max), BF16),
            pltpu.VMEM((6, cycles, order_max), BF16),
            pltpu.VMEM((chunks, depth, cols, width), BF16),
            pltpu.VMEM((chunks, 2, cols, width), BF16),
            pltpu.VMEM((3, cycles, span), BF16),
            pltpu.VMEM((6, cycles, span), BF16),
            pltpu.VMEM((8, cycles, span), BF16),
            dma((chunks + 3,)),
            dma((chunks, depth)),
            dma((chunks, depth)),
            dma((chunks, depth)),
            dma((chunks,)),
            dma((chunks,)),
            dma((chunks, 2)),
            dma((chunks,)),
            dma((2,)),
            dma((2,)),
            dma((2, far)),
            dma((2, far)),
            dma((2,)),
            dma((2,)),
            dma((2,)),
            dma((1,)),
            dma((2,)),
            dma((6,)),
            dma((6,)),
        ],
        compiler_params=pltpu.CompilerParams(collective_id=0, has_side_effects=True, vmem_limit_bytes=40 << 20),
        name="harmonics",
    )(keep(m_list), keep(coeff), keep(blocks), keep(legendre.reshape(rows_in, order_max)))
    tiles = 8
    sky = pl.pallas_call(
        functools.partial(synthesis_kernel, tiles, 1.0 / math.sqrt(subset)),
        out_shape=jax.ShapeDtypeStruct((rows_out, NPHI), BF16),
        in_specs=[vmem, vmem],
        out_specs=hbm,
        scratch_shapes=[
            pltpu.VMEM((rows_out, NPHI), BF16),
            dma((tiles,)),
        ],
        name="synthesis", compiler_params=pltpu.CompilerParams(vmem_limit_bytes=40 << 20),
    )(harmonics, table)
    return sky.reshape(cycles, REAL, NPHI)


def solution(mesh):
    spec = P(("groups", "mset"), None, None)
    return jax.shard_map(
        functools.partial(body, mesh.shape["mset"]),
        mesh=mesh,
        in_specs=(P(), spec, spec, spec),
        out_specs=spec,
        check_vma=False,
    )
```
